32 devices in a mesh: seg: 8 (over z, y), col: 4 (over x, core).
Axes of the slice: x: 2, y: 2, z: 4, core: 2. Of those that a mesh axis runs over, the one named last changes fastest.
Arguments:
- left_image: bfloat16 [65536, 2048], P('seg', 'col'), may hold values from -130 to 130
- right_image: bfloat16 [65536, 2048], P('seg', 'col'), may hold values from -130 to 130
- peak_offsets: int32 [2, 128, 4], P(None, 'seg', 'col'), may hold values from -15 to 15
- match_owner: int32 [114688, 1], P(('seg', 'col')), may hold values from 0 to 31; in each aligned block of 3584 rows (0 to 3583, 3584 to 7167, ...) at most 280 rows name the same one
- match_source: int32 [114688], P(('seg', 'col')), may hold values from 0 to 8191
- match_line: int32 [114688], P(('seg', 'col')), may hold values from 0 to 2047
Outputs:
- diag_blocks: float32 [6, 16384], P(None, ('seg', 'col'))
- coupling_blocks: float32 [6, 16384], P(None, ('seg', 'col'))
- normal_rhs: float32 [3, 16384], P(None, ('seg', 'col'))
The draws below stay inside these ranges and needn't reach their ends.
Inputs may be any that keep to these rules, and one draw needn't show every extreme that they name: `match_owner`: among the rows of one device, no owner is named by more than 280 matches.
All inputs are finite; a program needn't handle non-finite values.
Results may differ from the reference program's by a relative error of at most 0.0003.
Values may be sent and summed in bfloat16 or wider, within the bound.
A program may use at most 128 MiB of HBM per device.

```python
import math
import jax
import jax.numpy as jnp
import numpy as np
from jax import lax

TILE = 512
RANGE = 15
SAMP = 4
TROWS = 16
M_DEV = 3584
LINES_DEV = 8192
NL = 65536
NP = 2048
MATCHES = 114688
CAP = 280
SAMP_OWN = 512
LINES_OWN = 2048
NSAMP = 16384
N_COL = 4
DEVICES = 32


def joint_field(key):
    offset_key = jax.random.fold_in(key, 101)
    step_key = jax.random.fold_in(key, 102)
    field_key = jax.random.fold_in(key, 103)
    line_key = jax.random.fold_in(key, 104)
    column_key = jax.random.fold_in(key, 106)
    tile_rows = NL // TILE
    tile_cols = NP // TILE
    offsets = jax.random.randint(offset_key, (2, tile_rows, tile_cols), -RANGE, RANGE + 1).astype(jnp.int32)
    step_table = jax.random.randint(step_key, (tile_rows, tile_cols), 0, 9).astype(jnp.int32)
    background = jnp.clip(jax.random.normal(field_key, (NL, NP), jnp.float32), -4.0, 4.0)
    line_scale = jnp.exp(jax.random.uniform(line_key, (NL, 1), jnp.float32, 0.0, math.log(10.0)))
    column_scale = jnp.exp(jax.random.uniform(column_key, (1, NP), jnp.float32, 0.0, math.log(3.0)))
    first_strip = background * line_scale * column_scale
    return (first_strip, offsets, step_table)


def draw_left_image(key, part):
    first_strip, offsets, step_table = joint_field(key)
    return first_strip.astype(jnp.bfloat16)


def draw_peak_offsets(key, part):
    first_strip, offsets, step_table = joint_field(key)
    return offsets


def draw_right_image(key, part):
    first_strip, offsets, step_table = joint_field(key)
    noise_key = jax.random.fold_in(key, 105)
    noise = jnp.clip(jax.random.normal(noise_key, (NL, NP), jnp.float32), -4.0, 4.0)
    rim_width = RANGE + 1
    padded = jnp.pad(first_strip, rim_width, mode='wrap')
    tile_cols = NP // TILE

    def one_tile(tile_index):
        tile_row = tile_index // tile_cols
        tile_col = tile_index % tile_cols
        shift_row = offsets[0, tile_row, tile_col]
        shift_col = offsets[1, tile_row, tile_col]
        step_code = step_table[tile_row, tile_col]
        top_edge = tile_row * TILE + rim_width - shift_row
        left_edge = tile_col * TILE + rim_width - shift_col
        primary = lax.dynamic_slice(padded, (top_edge, left_edge), (TILE, TILE))
        secondary = lax.dynamic_slice(padded, (top_edge - step_code // 3 + 1, left_edge - step_code % 3 + 1), (TILE, TILE))
        return 0.6 * primary + 0.4 * secondary
    tiles = lax.map(one_tile, jnp.arange(NL // TILE * tile_cols, dtype=jnp.int32))
    mixed = tiles.reshape(NL // TILE, tile_cols, TILE, TILE).transpose(0, 2, 1, 3).reshape(NL, NP)
    return (mixed + 0.3 * noise).astype(jnp.bfloat16)


def touch_ends(array, stream_key, smallest, top_value):
    place = [jax.random.randint(jax.random.fold_in(stream_key, axis), (), 0, length) for axis, length in enumerate(array.shape)]
    widest = array.shape.index(max(array.shape))
    next_to = place[:widest] + [(place[widest] + 1) % array.shape[widest]] + place[widest + 1:]
    return array.at[tuple(place)].set(smallest).at[tuple(next_to)].set(top_value)


def routed_block(stream_key, own, number, rows, number_of, top, bound, lean):
    ranking = jax.random.permutation(stream_key, number_of)
    packed, common = load_shares(number_of, rows * top, bound, lean, True), load_shares(number_of, rows * top, bound, lean, False)
    places = jnp.arange(number_of)

    def named(sizes, offset_by):
        used = int((sizes > 0).sum())
        fixed = max(1, used // 4)
        passed = fixed + (places - fixed + offset_by * (used - fixed)) % max(1, number_of - fixed)
        return jnp.zeros((number_of,), jnp.int32).at[ranking[jnp.where(places < fixed, places, passed)]].set(jnp.asarray(sizes, jnp.int32))

    sizes = jnp.where(number % 4 == 0, named(packed, number // 4), named(common, number - number // 4 - 1))
    mixed = jax.random.permutation(jax.random.fold_in(own, 3), number_of)
    donor, sink = mixed[0:number_of // 2 * 2:2], mixed[1:number_of // 2 * 2:2]
    room = jnp.minimum(sizes[donor] - 1, bound - sizes[sink]) // 2
    room = jnp.where((donor == ranking[0]) | (sink == ranking[0]) | (sizes[sink] == 0), 0, jnp.maximum(room, 0))
    passed = jax.random.randint(jax.random.fold_in(own, 4), (number_of // 2,), 0, 1 << 20) % (room + 1)
    sizes = sizes.at[donor].add(-passed).at[sink].add(passed)
    members = jnp.searchsorted(jnp.cumsum(sizes), jnp.arange(rows * top), side="right").astype(jnp.int32)
    grid = members.reshape(top, rows).T
    grid = grid[jax.random.permutation(jax.random.fold_in(own, 1), rows)]
    offset_by = jax.random.randint(jax.random.fold_in(own, 2), (rows, 1), 0, top)
    return jnp.take_along_axis(grid, (jnp.arange(top)[None, :] + offset_by) % top, axis=1)


def load_shares(number_of, total, reach, skew, full):
    portions = [(1 << 20) // math.isqrt(standing ** skew) + 1 for standing in range(1, number_of + 1)]
    largest = reach if full else min(reach, max(-(-total // number_of), total * portions[0] // sum(portions)))
    least = 1 if total - largest >= number_of - 1 else 0
    holding, spare = [largest] + [least] * (number_of - 1), total - largest - least * (number_of - 1)
    while spare > 0:
        candidates = [i for i in range(1, number_of) if holding[i] < largest] or [i for i in range(1, number_of) if holding[i] < reach]
        pool, left = sum([portions[i] for i in candidates]), spare
        for i in candidates:
            addition = min(reach - holding[i], max(1, left * portions[i] // pool), spare)
            holding[i] = holding[i] + addition
            spare = spare - addition
    return np.array(holding)


def setup_inputs(seed: int = 0) -> dict:
    keys = jax.random.split(jax.random.key(seed), 7)
    left_image = draw_left_image(jax.random.fold_in(keys[6], 71), 0)
    right_image = draw_right_image(jax.random.fold_in(keys[6], 71), 0)
    peak_offsets = draw_peak_offsets(jax.random.fold_in(keys[6], 71), 0)
    match_owner_keys = jax.random.split(jax.random.fold_in(keys[3], 1), MATCHES // M_DEV)
    match_owner_turns = jax.random.permutation(jax.random.fold_in(keys[3], 3), MATCHES // M_DEV)
    match_owner = jax.vmap(lambda own, number: routed_block(jax.random.fold_in(keys[3], 2), own, number, M_DEV, DEVICES, 1, CAP, 1))(match_owner_keys, match_owner_turns).reshape((MATCHES, 1))
    match_source = touch_ends(jax.random.randint(keys[4], (MATCHES,), 0, LINES_DEV), jax.random.fold_in(keys[4], 1), 0, LINES_DEV - 1).astype(jnp.int32)
    match_line = touch_ends(jax.random.randint(keys[5], (MATCHES,), 0, LINES_OWN), jax.random.fold_in(keys[5], 1), 0, LINES_OWN - 1).astype(jnp.int32)
    return dict(left_image=left_image, right_image=right_image, peak_offsets=peak_offsets, match_owner=match_owner, match_source=match_source, match_line=match_line)


EPSILON = 1e-05
SHARPNESS = 6.0
JACOBIAN_A = 0.5
JACOBIAN_B = -0.3
JACOBIAN_C = -0.8

def tile_observations(window, left_tile, offset_row, offset_col):
    tile_lines = left_tile.shape[0]
    pixels = left_tile.shape[1]
    pixel_count = float(pixels)
    left_vals = left_tile.astype(jnp.float32)
    left_sum = lax.optimization_barrier(jnp.sum(left_vals, axis=1))
    left_var = lax.optimization_barrier(jnp.sum(left_vals * left_vals, axis=1)) - left_sum * left_sum / pixel_count + pixel_count * EPSILON
    table = {}
    for col_step in range(3):
        right_cols = window[:, col_step:col_step + pixels].astype(jnp.float32)
        line_sum = lax.optimization_barrier(jnp.sum(right_cols, axis=1))
        line_square = lax.optimization_barrier(jnp.sum(right_cols * right_cols, axis=1))
        for row_step in range(3):
            right_vals = right_cols[row_step:row_step + tile_lines]
            right_sum = line_sum[row_step:row_step + tile_lines]
            right_var = line_square[row_step:row_step + tile_lines] - right_sum * right_sum / pixel_count + pixel_count * EPSILON
            covariance = lax.optimization_barrier(jnp.sum(left_vals * right_vals, axis=1)) - left_sum * right_sum / pixel_count
            table[row_step, col_step] = covariance / jnp.sqrt(left_var * right_var)
    scores = jnp.stack([table[row_step, col_step] for row_step in range(3) for col_step in range(3)])
    exp_scores = jnp.exp(SHARPNESS * scores)
    denominator = lax.optimization_barrier(jnp.sum(exp_scores, axis=0))
    shift_row = (lax.optimization_barrier(jnp.sum(exp_scores[6:], axis=0)) - lax.optimization_barrier(jnp.sum(exp_scores[:3], axis=0))) / denominator
    shift_col = (lax.optimization_barrier(jnp.sum(exp_scores[2::3], axis=0)) - lax.optimization_barrier(jnp.sum(exp_scores[0::3], axis=0))) / denominator
    offset_scale = 1.0 / (RANGE + 1)
    resid_row = (offset_row.astype(jnp.float32) + shift_row) * offset_scale
    resid_col = (offset_col.astype(jnp.float32) + shift_col) * offset_scale
    weight = 0.2 * (0.1 + scores[4] * scores[4])
    return jnp.stack([resid_row, resid_col, weight])

def normal_terms(resid_row, resid_col, weight, spread):
    unity = jnp.ones_like(spread)
    along_track = [JACOBIAN_A * spread, unity, spread]
    across = [unity, JACOBIAN_B * spread, JACOBIAN_C * spread]
    index_pairs = ((0, 0), (0, 1), (0, 2), (1, 1), (1, 2), (2, 2))
    moment = jnp.stack([weight * (along_track[first_index] * along_track[second_index] + across[first_index] * across[second_index]) for first_index, second_index in index_pairs], axis=0)
    gradient = jnp.stack([weight * (along_track[first_index] * resid_row + across[first_index] * resid_col) for first_index in range(3)], axis=0)
    return (moment, gradient)

def line_fraction(line_ids):
    return ((line_ids % SAMP).astype(jnp.float32) + 0.5) / SAMP

def bin_terms(moment, gradient, sample_ids, fraction, bin_count):
    near_weight = 1.0 - fraction
    next_ids = sample_ids + 1
    diagonal = jnp.zeros((6, bin_count), jnp.float32).at[:, sample_ids].add(moment * (near_weight * near_weight)[None, :], mode='drop')
    diagonal = diagonal.at[:, next_ids].add(moment * (fraction * fraction)[None, :], mode='drop')
    coupling = jnp.zeros((6, bin_count), jnp.float32).at[:, sample_ids].add(moment * (fraction * near_weight)[None, :], mode='drop')
    right_side = jnp.zeros((3, bin_count), jnp.float32).at[:, sample_ids].add(gradient * near_weight[None, :], mode='drop')
    right_side = right_side.at[:, next_ids].add(gradient * fraction[None, :], mode='drop')
    return (diagonal, coupling, right_side)

def reference(left_image, right_image, peak_offsets, match_owner, match_source, match_line):
    rim_width = RANGE + 1
    padded = jnp.pad(right_image, rim_width)
    tile_cols = NP // TILE

    def one_tile(tile_index):
        tile_row = tile_index // tile_cols
        tile_col = tile_index % tile_cols
        offset_row = peak_offsets[0, tile_row, tile_col]
        offset_col = peak_offsets[1, tile_row, tile_col]
        window = lax.dynamic_slice(padded, (tile_row * TILE + rim_width + offset_row - 1, tile_col * TILE + rim_width + offset_col - 1), (TILE + 2, TILE + 2))
        left_tile = lax.dynamic_slice(left_image, (tile_row * TILE, tile_col * TILE), (TILE, TILE))
        return tile_observations(window, left_tile, offset_row, offset_col)
    observations = lax.map(one_tile, jnp.arange(NL // TILE * tile_cols, dtype=jnp.int32))
    device = jnp.arange(MATCHES, dtype=jnp.int32) // M_DEV
    segment = device // N_COL
    column = device % N_COL
    tile_index = (segment * TROWS + match_source // TILE) * N_COL + column
    records = observations[tile_index, :, match_source % TILE]
    spread = 2.0 * (column.astype(jnp.float32) + 0.5) / N_COL - 1.0
    moment, gradient = normal_terms(records[:, 0], records[:, 1], records[:, 2], spread)
    sample_ids = match_owner[:, 0] * SAMP_OWN + match_line // SAMP
    diag_blocks, coupling_blocks, normal_rhs = bin_terms(moment, gradient, sample_ids, line_fraction(match_line), NSAMP)
    return (diag_blocks, coupling_blocks, normal_rhs)
```

```python
import functools

import jax
import jax.numpy as jnp
from jax import lax
from jax.experimental import pallas as pl
from jax.experimental.pallas import tpu as pltpu
from jax.sharding import PartitionSpec as P

TILE = 512
RANGE = 15
SAMP = 4
RIM = RANGE + 1
LANES = 128
WINDOW = TILE + 2 * RIM
PADDED = TILE + LANES

EPSILON = 1e-05
SHARPNESS = 6.0
JACOBIAN_A = 0.5
JACOBIAN_B = -0.3
JACOBIAN_C = -0.8

F32 = jnp.float32
BF16 = jnp.bfloat16


def iota(shape, dim):
    return lax.broadcasted_iota(jnp.int32, shape, dim)


def rim_rows(tile, tiles, prev_ref, next_ref, above_ref, below_ref):
    before = jnp.where(tile == 0, above_ref[...].astype(F32), prev_ref[...].astype(F32))
    after = jnp.where(tile == tiles - 1, below_ref[...].astype(F32), next_ref[...].astype(F32))
    return before, after


def edge_kernel(tiles, *refs):
    sides, outs = (refs[:5], refs[5:10]), refs[10:]
    tile = pl.program_id(0)
    for side in range(2):
        main_ref, prev_ref, next_ref, above_ref, below_ref = sides[side]
        before, after = rim_rows(tile, tiles, prev_ref, next_ref, above_ref, below_ref)
        wrap = jnp.concatenate(
            [after, jnp.zeros((LANES - 2 * RIM, LANES), F32), before], axis=0
        ).astype(BF16)
        first = 0 if side == 0 else LANES - RIM
        pick = (iota((RIM, LANES), 1) == iota((RIM, LANES), 0) + first).astype(F32).astype(BF16)
        contract = (((1,), (1,)), ((), ()))
        main = lax.dot_general(pick, main_ref[...], contract, preferred_element_type=F32)
        rest = lax.dot_general(pick, wrap, contract, preferred_element_type=F32)
        outs[side][0, :, :TILE] = main.astype(BF16)
        outs[side][0, :, TILE:] = rest.astype(BF16)


def edges(right, above, below):
    lines, pixels = right.shape
    tiles, blocks, per = lines // TILE, lines // RIM, TILE // RIM
    specs, operands = [], []
    for block in (0, pixels // LANES - 1):
        specs += [
            pl.BlockSpec((TILE, LANES), lambda t, block=block: (t, block)),
            pl.BlockSpec((RIM, LANES), lambda t, block=block: (jnp.maximum(t * per - 1, 0), block)),
            pl.BlockSpec(
                (RIM, LANES),
                lambda t, block=block: (jnp.minimum((t + 1) * per, blocks - 1), block),
            ),
            pl.BlockSpec((RIM, LANES), lambda t, block=block: (0, block)),
            pl.BlockSpec((RIM, LANES), lambda t, block=block: (0, block)),
        ]
        operands += [right, right, right, above, below]
    out = jax.ShapeDtypeStruct((tiles, RIM, PADDED), BF16)
    return pl.pallas_call(
        functools.partial(edge_kernel, tiles),
        grid=(tiles,),
        in_specs=specs,
        out_specs=[pl.BlockSpec((1, RIM, PADDED), lambda t: (t, 0, 0))] * 2,
        out_shape=[out, out],
        name="edges",
    )(*operands)


def pick_lines(load, count):
    lane = iota((8, LANES), 1)
    group = lane // 8
    acc = load(0)
    for i in range(1, count):
        acc = jnp.where(group == i, load(i), acc)
    acc = jnp.where(lane % 8 == iota((8, LANES), 0), acc, 0.0)
    return jnp.sum(acc, axis=0, keepdims=True)


def correlate_kernel(
    tiles,
    offsets_ref,
    left_ref,
    main_ref,
    prev_ref,
    next_ref,
    above_ref,
    below_ref,
    west_ref,
    east_ref,
    out_ref,
    shifted_ref,
    halo_ref,
    stat_ref,
    flat_ref,
    gram_ref,
    dots_ref,
    sums_ref,
    squares_ref,
):
    tile = pl.program_id(0)
    offset_row = offsets_ref[0, tile]
    offset_col = offsets_ref[1, tile]
    blocks = TILE // LANES

    contract = (((0,), (0,)), ((), ()))
    spot = iota((RIM, LANES), 1) - iota((RIM, LANES), 0)
    east = lax.dot_general(
        east_ref[0], (spot == 0).astype(F32).astype(BF16), contract, preferred_element_type=F32
    )
    west = lax.dot_general(
        west_ref[0],
        (spot == LANES - RIM).astype(F32).astype(BF16),
        contract,
        preferred_element_type=F32,
    )
    halo_ref[...] = east + west

    def process(values, halo, target):
        rows = values.shape[0]
        parts = [values[:, LANES * b : LANES * (b + 1)] for b in range(blocks)] + [halo]
        lane = iota((rows, LANES), 1)
        for s in range(3):
            step = offset_col + (s - 1)
            turn = lax.rem(LANES - step, LANES)
            turned = [pltpu.roll(part, turn, 1) for part in parts]
            source = lane + step
            low, high = source < 0, source >= LANES
            total = squares = None
            for b in range(blocks):
                value = jnp.where(
                    low, turned[b - 1], jnp.where(high, turned[b + 1], turned[b])
                )
                total = value if b == 0 else total + value
                squares = value * value if b == 0 else squares + value * value
                shifted_ref[s, pl.ds(target, rows), LANES * b : LANES * (b + 1)] = value.astype(BF16)
            stat_ref[s, pl.ds(target, rows), :] = jnp.broadcast_to(
                jnp.sum(total, axis=1, keepdims=True), (rows, LANES)
            )
            stat_ref[3 + s, pl.ds(target, rows), :] = jnp.broadcast_to(
                jnp.sum(squares, axis=1, keepdims=True), (rows, LANES)
            )

    before, after = rim_rows(tile, tiles, prev_ref, next_ref, above_ref, below_ref)
    process(before, halo_ref[PADDED - RIM :, :], 0)
    process(after, halo_ref[TILE : TILE + RIM, :], RIM + TILE)
    chunk = 32

    @pl.loop(0, TILE // chunk)
    def _(index):
        start = pl.multiple_of(index * chunk, chunk)
        process(
            main_ref[pl.ds(start, chunk), :].astype(F32),
            halo_ref[pl.ds(start, chunk), :],
            pl.multiple_of(start + RIM, RIM),
        )
        left = left_ref[pl.ds(start, chunk), :].astype(F32)
        parts = [left[:, LANES * b : LANES * (b + 1)] for b in range(blocks)]
        total = parts[0] + parts[1] + parts[2] + parts[3]
        squares = sum(part * part for part in parts[1:]) + parts[0] * parts[0]
        stat_ref[6, pl.ds(start, chunk), :] = jnp.broadcast_to(
            jnp.sum(total, axis=1, keepdims=True), (chunk, LANES)
        )
        stat_ref[7, pl.ds(start, chunk), :] = jnp.broadcast_to(
            jnp.sum(squares, axis=1, keepdims=True), (chunk, LANES)
        )

    for k in range(8):
        for b in range(5 if k < 6 else 4):
            flat_ref[k : k + 1, LANES * b : LANES * (b + 1)] = pick_lines(
                lambda i: stat_ref[k, LANES * b + 8 * i : LANES * b + 8 * i + 8, :],
                16 if b < 4 else 4,
            )

    lane = iota((8, LANES), 1)
    for r in range(3):
        start = offset_row + (RANGE + r)
        turn = lax.rem(LANES - start, LANES)
        turned = [
            pltpu.roll(flat_ref[:, LANES * b : LANES * (b + 1)], turn, 1) for b in range(blocks + 1)
        ]
        for b in range(blocks):
            value = jnp.where(lane < LANES - start, turned[b], turned[b + 1])
            sums_ref[3 * r : 3 * r + 3, LANES * b : LANES * (b + 1)] = value[0:3]
            squares_ref[3 * r : 3 * r + 3, LANES * b : LANES * (b + 1)] = value[3:6]

    for b in range(blocks):
        for s in range(3):
            gram_ref[b, s] = lax.dot_general(
                shifted_ref[s, LANES * b : LANES * b + LANES + 2 * RIM, :],
                left_ref[LANES * b : LANES * (b + 1), :],
                (((1,), (1,)), ((), ())),
                preferred_element_type=F32,
            )
        for r in range(3):
            start = offset_row + (RANGE + r)
            for s in range(3):
                dots_ref[3 * r + s : 3 * r + s + 1, LANES * b : LANES * (b + 1)] = pick_lines(
                    lambda i: gram_ref[b, s, pl.ds(start + 8 * i, 8), :], 16
                )

    count = float(TILE)
    left_sum = flat_ref[6:7, :TILE]
    left_var = flat_ref[7:8, :TILE] - left_sum * left_sum / count + count * EPSILON
    right_sum = sums_ref[0:9, :]
    right_var = squares_ref[0:9, :] - right_sum * right_sum / count + count * EPSILON
    covariance = dots_ref[0:9, :] - left_sum * right_sum / count
    scores = covariance / jnp.sqrt(left_var * right_var)
    weights = jnp.exp(SHARPNESS * scores)
    row = [weights[i : i + 1] for i in range(9)]
    denominator = sum(row[1:], row[0])
    shift_row = ((row[6] + row[7] + row[8]) - (row[0] + row[1] + row[2])) / denominator
    shift_col = ((row[2] + row[5] + row[8]) - (row[0] + row[3] + row[6])) / denominator
    scale = 1.0 / (RANGE + 1)
    out_ref[0, 0:1, :] = (offset_row.astype(F32) + shift_row) * scale
    out_ref[0, 1:2, :] = (offset_col.astype(F32) + shift_col) * scale
    out_ref[0, 2:3, :] = 0.2 * (0.1 + scores[4:5] * scores[4:5])


def correlate(offsets, left, right, above, below, west, east):
    lines, pixels = left.shape
    tiles, blocks, per = lines // TILE, lines // RIM, TILE // RIM
    rim = pl.BlockSpec((RIM, pixels), lambda t, o: (0, 0))
    side = pl.BlockSpec((1, RIM, PADDED), lambda t, o: (t, 0, 0))
    return pl.pallas_call(
        functools.partial(correlate_kernel, tiles),
        grid_spec=pltpu.PrefetchScalarGridSpec(
            num_scalar_prefetch=1,
            grid=(tiles,),
            in_specs=[
                pl.BlockSpec((TILE, pixels), lambda t, o: (t, 0)),
                pl.BlockSpec((TILE, pixels), lambda t, o: (t, 0)),
                pl.BlockSpec((RIM, pixels), lambda t, o: (jnp.maximum(t * per - 1, 0), 0)),
                pl.BlockSpec((RIM, pixels), lambda t, o: (jnp.minimum((t + 1) * per, blocks - 1), 0)),
                rim,
                rim,
                side,
                side,
            ],
            out_specs=pl.BlockSpec((1, 8, TILE), lambda t, o: (t, 0, 0)),
            scratch_shapes=[
                pltpu.VMEM((3, WINDOW, TILE), BF16),
                pltpu.VMEM((PADDED, LANES), F32),
                pltpu.VMEM((8, PADDED, LANES), F32),
                pltpu.VMEM((8, PADDED), F32),
                pltpu.VMEM((TILE // LANES, 3, LANES + 2 * RIM, LANES), F32),
                pltpu.VMEM((16, TILE), F32),
                pltpu.VMEM((16, TILE), F32),
                pltpu.VMEM((16, TILE), F32),
            ],
        ),
        out_shape=jax.ShapeDtypeStruct((tiles, 8, TILE), F32),
        name="correlate",
    )(offsets, left, right, right, right, above, below, west, east)


def bin_kernel(
    per_owner, obs_ref, owner_ref, source_ref, line_ref, out_ref, value_ref, spot_ref, hot_ref, part_ref, bins_ref
):
    tiles = obs_ref.shape[0]
    groups = owner_ref.shape[0] // 8
    match_rows = hot_ref.shape[1] // LANES
    bins = bins_ref.shape[1]
    sources = [source_ref[8 * g : 8 * g + 8, :] for g in range(groups)]
    high = [source // LANES for source in sources]
    low = [source % LANES for source in sources]
    fields = [[jnp.zeros((8, LANES), F32)] * groups for _ in range(3)]
    for t in range(tiles):
        for b in range(TILE // LANES):
            here = [h == t * (TILE // LANES) + b for h in high]
            for v in range(3):
                table = jnp.broadcast_to(
                    obs_ref[t, v : v + 1, LANES * b : LANES * (b + 1)], (8, LANES)
                )
                for g in range(groups):
                    taken = jnp.take_along_axis(table, low[g], axis=1, mode="promise_in_bounds")
                    fields[v][g] = jnp.where(here[g], taken, fields[v][g])
    for g in range(groups):
        rows = slice(8 * g, 8 * g + 8)
        line = line_ref[rows, :]
        far = ((line % SAMP).astype(F32) + 0.5) / SAMP
        near = 1.0 - far
        sample = owner_ref[rows, :] * per_owner + line // SAMP
        spot_ref[0, rows, :] = sample // LANES
        spot_ref[1, rows, :] = sample % LANES
        weight = fields[2][g]
        along, across = weight * fields[0][g], weight * fields[1][g]
        values = [
            weight * (near * near),
            weight * (far * far),
            weight * (far * near),
            along * near,
            along * far,
            across * near,
            across * far,
        ]
        for v in range(7):
            upper = values[v].astype(BF16).astype(F32)
            value_ref[v, 0, rows, :] = upper
            value_ref[v, 1, rows, :] = values[v] - upper
    for r in range(match_rows):
        hot = iota((LANES, LANES), 0) == spot_ref[1, r : r + 1, :]
        hot_ref[:, LANES * r : LANES * (r + 1)] = hot.astype(F32).astype(BF16)

    @pl.loop(0, 7)
    def _(v):
        for r in range(match_rows):
            here = iota((bins, LANES), 0) == spot_ref[0, r : r + 1, :]
            for p in range(2):
                part_ref[p, :, LANES * r : LANES * (r + 1)] = jnp.where(
                    here, value_ref[v, p, r : r + 1, :], 0.0
                ).astype(BF16)
        contract = (((1,), (1,)), ((), ()))
        bins_ref[v] = lax.dot_general(
            part_ref[0], hot_ref[...], contract, preferred_element_type=F32
        ) + lax.dot_general(part_ref[1], hot_ref[...], contract, preferred_element_type=F32)

    lane, row = iota((bins, LANES), 1), iota((bins, LANES), 0)
    for v in (1, 4, 6):
        turned = pltpu.roll(bins_ref[v], 1, 1)
        carried = jnp.where(row == 0, 0.0, pltpu.roll(turned, 1, 0))
        bins_ref[v - 1] = bins_ref[v - 1] + jnp.where(lane == 0, carried, turned)
    span = per_owner // LANES
    for d in range(bins // span):
        for i, v in enumerate((0, 2, 3, 5)):
            out_ref[d, span * i : span * (i + 1), :] = bins_ref[v, span * d : span * (d + 1), :]


def bin_matches(observations, owner, source, line, device_count, per_owner):
    count = source.shape[0]
    match_rows = count // LANES
    padded_rows = -(-match_rows // 8) * 8
    spare = padded_rows * LANES - count

    def lay(array, fill):
        return jnp.pad(array, (0, spare), constant_values=fill).reshape(padded_rows, LANES)

    bins = device_count * per_owner // LANES
    block = 4 * per_owner // LANES
    return pl.pallas_call(
        functools.partial(bin_kernel, per_owner),
        out_shape=jax.ShapeDtypeStruct((device_count, block, LANES), F32),
        scratch_shapes=[
            pltpu.VMEM((7, 2, padded_rows, LANES), F32),
            pltpu.VMEM((2, padded_rows, LANES), jnp.int32),
            pltpu.VMEM((LANES, match_rows * LANES), BF16),
            pltpu.VMEM((2, bins, match_rows * LANES), BF16),
            pltpu.VMEM((7, bins, LANES), F32),
        ],
        name="bin_matches",
    )(observations, lay(owner, 0), lay(source, 0), lay(line, 0))


def local(left_image, right_image, peak_offsets, match_owner, match_source, match_line):
    rows_dev = left_image.shape[0]
    seg_count = lax.axis_size("seg")
    col_count = lax.axis_size("col")
    device_count = seg_count * col_count
    samp_own = rows_dev // (SAMP * col_count)

    def forward(value, axis):
        size = lax.axis_size(axis)
        return lax.ppermute(value, axis, [(i, i + 1) for i in range(size - 1)])

    def backward(value, axis):
        size = lax.axis_size(axis)
        return lax.ppermute(value, axis, [(i + 1, i) for i in range(size - 1)])

    above = forward(right_image[rows_dev - RIM :], "seg")
    below = backward(right_image[:RIM], "seg")
    first_edge, last_edge = edges(right_image, above, below)
    west = forward(last_edge, "col")
    east = backward(first_edge, "col")
    observations = correlate(
        peak_offsets[:, :, 0], left_image, right_image, above, below, west, east
    )
    outgoing = bin_matches(
        observations, match_owner[:, 0], match_source, match_line, device_count, samp_own
    )
    received = lax.all_to_all(outgoing, ("seg", "col"), split_axis=0, concat_axis=0, tiled=True)
    by_column = jnp.sum(received.reshape(seg_count, col_count, 4, samp_own), axis=0)
    index_pairs = ((0, 0), (0, 1), (0, 2), (1, 1), (1, 2), (2, 2))
    diagonal, coupling, right_side = [0.0] * 6, [0.0] * 6, [0.0] * 3
    for column in range(col_count):
        spread = 2.0 * (column + 0.5) / col_count - 1.0
        along = (JACOBIAN_A * spread, 1.0, spread)
        across = (1.0, JACOBIAN_B * spread, JACOBIAN_C * spread)
        near, both, resid_row, resid_col = (by_column[column, i] for i in range(4))
        for i, (a, b) in enumerate(index_pairs):
            factor = along[a] * along[b] + across[a] * across[b]
            diagonal[i] = diagonal[i] + factor * near
            coupling[i] = coupling[i] + factor * both
        for a in range(3):
            right_side[a] = right_side[a] + along[a] * resid_row + across[a] * resid_col
    return (jnp.stack(diagonal), jnp.stack(coupling), jnp.stack(right_side))


def solution(mesh):
    return jax.shard_map(
        local,
        mesh=mesh,
        in_specs=(
            P("seg", "col"),
            P("seg", "col"),
            P(None, "seg", "col"),
            P(("seg", "col"), None),
            P(("seg", "col")),
            P(("seg", "col")),
        ),
        out_specs=(P(None, ("seg", "col")), P(None, ("seg", "col")), P(None, ("seg", "col"))),
        check_vma=False,
    )
```

```python
import functools

import jax
import jax.numpy as jnp
from jax import lax
from jax.experimental import pallas as pl
from jax.experimental.pallas import tpu as pltpu
from jax.sharding import PartitionSpec as P

TILE = 512
RANGE = 15
SAMP = 4
RIM = RANGE + 1
LANES = 128
WINDOW = TILE + 2 * RIM
PADDED = TILE + LANES

EPSILON = 1e-05
SHARPNESS = 6.0
JACOBIAN_A = 0.5
JACOBIAN_B = -0.3
JACOBIAN_C = -0.8

F32 = jnp.float32
BF16 = jnp.bfloat16


def iota(shape, dim):
    return lax.broadcasted_iota(jnp.int32, shape, dim)


def rim_rows(tile, tiles, prev_ref, next_ref, above_ref, below_ref):
    before = jnp.where(tile == 0, above_ref[...].astype(F32), prev_ref[...].astype(F32))
    after = jnp.where(tile == tiles - 1, below_ref[...].astype(F32), next_ref[...].astype(F32))
    return before, after


def edge_kernel(steps, per_step, *refs):
    sides, outs = (refs[:5], refs[5:10]), refs[10:]
    step = pl.program_id(0)
    contract = (((1,), (1,)), ((), ()))
    for side in range(2):
        main_ref, prev_ref, next_ref, above_ref, below_ref = sides[side]
        before, after = rim_rows(step, steps, prev_ref, next_ref, above_ref, below_ref)
        first = 0 if side == 0 else LANES - RIM
        pick = (iota((RIM, LANES), 1) == iota((RIM, LANES), 0) + first).astype(F32).astype(BF16)
        zeros = jnp.zeros((LANES - 2 * RIM, LANES), F32)
        for tile in range(per_step):
            start = tile * TILE
            head = before if tile == 0 else main_ref[start - RIM : start, :].astype(F32)
            stop = start + TILE
            tail = after if tile == per_step - 1 else main_ref[stop : stop + RIM, :].astype(F32)
            wrap = jnp.concatenate([tail, zeros, head], axis=0).astype(BF16)
            main = lax.dot_general(
                pick, main_ref[start:stop, :], contract, preferred_element_type=F32
            )
            rest = lax.dot_general(pick, wrap, contract, preferred_element_type=F32)
            outs[side][tile, :, :TILE] = main.astype(BF16)
            outs[side][tile, :, TILE:] = rest.astype(BF16)


def edges(right, above, below):
    lines, pixels = right.shape
    tiles, blocks = lines // TILE, lines // RIM
    per_step = 4 if tiles % 4 == 0 else 1
    steps, per = tiles // per_step, per_step * TILE // RIM
    specs, operands = [], []
    for block in (0, pixels // LANES - 1):
        specs += [
            pl.BlockSpec((per_step * TILE, LANES), lambda t, block=block: (t, block)),
            pl.BlockSpec((RIM, LANES), lambda t, block=block: (jnp.maximum(t * per - 1, 0), block)),
            pl.BlockSpec(
                (RIM, LANES),
                lambda t, block=block: (jnp.minimum((t + 1) * per, blocks - 1), block),
            ),
            pl.BlockSpec((RIM, LANES), lambda t, block=block: (0, block)),
            pl.BlockSpec((RIM, LANES), lambda t, block=block: (0, block)),
        ]
        operands += [right, right, right, above, below]
    out = jax.ShapeDtypeStruct((tiles, RIM, PADDED), BF16)
    return pl.pallas_call(
        functools.partial(edge_kernel, steps, per_step),
        grid=(steps,),
        in_specs=specs,
        out_specs=[pl.BlockSpec((per_step, RIM, PADDED), lambda t: (t, 0, 0))] * 2,
        out_shape=[out, out],
        name="edges",
    )(*operands)


def pick_lines(load, count):
    lane = iota((8, LANES), 1)
    group = lane // 8
    acc = load(0)
    for i in range(1, count):
        acc = jnp.where(group == i, load(i), acc)
    acc = jnp.where(lane % 8 == iota((8, LANES), 0), acc, 0.0)
    return jnp.sum(acc, axis=0, keepdims=True)


def correlate_kernel(
    tiles,
    offsets_ref,
    left_ref,
    main_ref,
    prev_ref,
    next_ref,
    above_ref,
    below_ref,
    west_ref,
    east_ref,
    out_ref,
    shifted_ref,
    halo_ref,
    window_ref,
    window_square_ref,
    left_square_ref,
    flat_ref,
    gram_ref,
    dots_ref,
    sums_ref,
    squares_ref,
):
    tile = pl.program_id(0)
    offset_row = offsets_ref[0, tile]
    offset_col = offsets_ref[1, tile]
    blocks = TILE // LANES

    contract = (((0,), (0,)), ((), ()))
    spot = iota((RIM, LANES), 1) - iota((RIM, LANES), 0)
    east = lax.dot_general(
        east_ref[0], (spot == 0).astype(F32).astype(BF16), contract, preferred_element_type=F32
    )
    west = lax.dot_general(
        west_ref[0],
        (spot == LANES - RIM).astype(F32).astype(BF16),
        contract,
        preferred_element_type=F32,
    )
    halo_ref[...] = (east + west).astype(BF16)

    def split_squares(values, square_ref, target, place):
        rows, width = values.shape
        square = values.astype(F32) * values.astype(F32)
        upper = square.astype(BF16)
        square_ref[0, pl.ds(target, rows), place : place + width] = upper
        square_ref[1, pl.ds(target, rows), place : place + width] = (
            square - upper.astype(F32)
        ).astype(BF16)

    def process(values, halo, target):
        rows = values.shape[0]
        parts = [values[:, LANES * b : LANES * (b + 1)] for b in range(blocks)] + [halo]
        for b in range(blocks + 1):
            window_ref[pl.ds(target, rows), LANES * b : LANES * (b + 1)] = parts[b]
            split_squares(parts[b], window_square_ref, target, LANES * b)
        lane = iota((rows, LANES), 1)
        for s in range(3):
            step = offset_col + (s - 1)
            turn = lax.rem(LANES - step, LANES)
            turned = [pltpu.roll(part, turn, 1) for part in parts]
            source = lane + step
            low, high = source < 0, source >= LANES
            for b in range(blocks):
                shifted_ref[s, pl.ds(target, rows), LANES * b : LANES * (b + 1)] = jnp.where(
                    low, turned[b - 1], jnp.where(high, turned[b + 1], turned[b])
                )

    before, after = rim_rows(tile, tiles, prev_ref, next_ref, above_ref, below_ref)
    process(before.astype(BF16), halo_ref[PADDED - RIM :, :], 0)
    process(after.astype(BF16), halo_ref[TILE : TILE + RIM, :], RIM + TILE)
    chunk = 64

    @pl.loop(0, TILE // chunk)
    def _(index):
        start = pl.multiple_of(index * chunk, chunk)
        process(
            main_ref[pl.ds(start, chunk), :],
            halo_ref[pl.ds(start, chunk), :],
            pl.multiple_of(start + RIM, RIM),
        )
        split_squares(left_ref[pl.ds(start, chunk), :], left_square_ref, start, 0)

    def mask_rows(width, first, last):
        row, pixel = iota((16, width), 0), iota((16, width), 1)
        place = pixel - (offset_col - 1 + row % 3)
        place = jnp.where(place < 0, place + PADDED, place)
        place = jnp.where(place >= PADDED, place - PADDED, place)
        inside = (place < TILE) & (row >= first) & (row < last)
        return inside.astype(F32).astype(BF16)

    def line_sums(mask, lines):
        return lax.dot_general(mask, lines, (((1,), (1,)), ((), ())), preferred_element_type=F32)

    sum_mask, square_mask = mask_rows(PADDED, 0, 3), mask_rows(PADDED, 3, 6)
    flat_ref[...] = (
        line_sums(sum_mask, window_ref[...])
        + line_sums(square_mask, window_square_ref[0])
        + line_sums(square_mask, window_square_ref[1])
    )
    row = iota((16, TILE), 0)
    left_sums = (
        line_sums((row == 0).astype(F32).astype(BF16), left_ref[...])
        + line_sums((row == 1).astype(F32).astype(BF16), left_square_ref[0])
        + line_sums((row == 1).astype(F32).astype(BF16), left_square_ref[1])
    )

    lane = iota((8, LANES), 1)
    for r in range(3):
        start = offset_row + (RANGE + r)
        turn = lax.rem(LANES - start, LANES)
        turned = [
            pltpu.roll(flat_ref[0:8, LANES * b : LANES * (b + 1)], turn, 1) for b in range(blocks + 1)
        ]
        for b in range(blocks):
            value = jnp.where(lane < LANES - start, turned[b], turned[b + 1])
            sums_ref[3 * r : 3 * r + 3, LANES * b : LANES * (b + 1)] = value[0:3]
            squares_ref[3 * r : 3 * r + 3, LANES * b : LANES * (b + 1)] = value[3:6]

    for b in range(blocks):
        for s in range(3):
            gram_ref[b, s] = lax.dot_general(
                shifted_ref[s, LANES * b : LANES * b + LANES + 2 * RIM, :],
                left_ref[LANES * b : LANES * (b + 1), :],
                (((1,), (1,)), ((), ())),
                preferred_element_type=F32,
            )
        for r in range(3):
            start = offset_row + (RANGE + r)
            for s in range(3):
                dots_ref[3 * r + s : 3 * r + s + 1, LANES * b : LANES * (b + 1)] = pick_lines(
                    lambda i: gram_ref[b, s, pl.ds(start + 8 * i, 8), :], 16
                )

    count = float(TILE)
    left_sum = left_sums[0:1]
    left_var = left_sums[1:2] - left_sum * left_sum / count + count * EPSILON
    right_sum = sums_ref[0:9, :]
    right_var = squares_ref[0:9, :] - right_sum * right_sum / count + count * EPSILON
    covariance = dots_ref[0:9, :] - left_sum * right_sum / count
    scores = covariance / jnp.sqrt(left_var * right_var)
    weights = jnp.exp(SHARPNESS * scores)
    row = [weights[i : i + 1] for i in range(9)]
    denominator = sum(row[1:], row[0])
    shift_row = ((row[6] + row[7] + row[8]) - (row[0] + row[1] + row[2])) / denominator
    shift_col = ((row[2] + row[5] + row[8]) - (row[0] + row[3] + row[6])) / denominator
    scale = 1.0 / (RANGE + 1)
    out_ref[0, 0:1, :] = (offset_row.astype(F32) + shift_row) * scale
    out_ref[0, 1:2, :] = (offset_col.astype(F32) + shift_col) * scale
    out_ref[0, 2:3, :] = 0.2 * (0.1 + scores[4:5] * scores[4:5])


def correlate(offsets, left, right, above, below, west, east):
    lines, pixels = left.shape
    tiles, blocks, per = lines // TILE, lines // RIM, TILE // RIM
    rim = pl.BlockSpec((RIM, pixels), lambda t, o: (0, 0))
    side = pl.BlockSpec((1, RIM, PADDED), lambda t, o: (t, 0, 0))
    return pl.pallas_call(
        functools.partial(correlate_kernel, tiles),
        grid_spec=pltpu.PrefetchScalarGridSpec(
            num_scalar_prefetch=1,
            grid=(tiles,),
            in_specs=[
                pl.BlockSpec((TILE, pixels), lambda t, o: (t, 0)),
                pl.BlockSpec((TILE, pixels), lambda t, o: (t, 0)),
                pl.BlockSpec((RIM, pixels), lambda t, o: (jnp.maximum(t * per - 1, 0), 0)),
                pl.BlockSpec((RIM, pixels), lambda t, o: (jnp.minimum((t + 1) * per, blocks - 1), 0)),
                rim,
                rim,
                side,
                side,
            ],
            out_specs=pl.BlockSpec((1, 8, TILE), lambda t, o: (t, 0, 0)),
            scratch_shapes=[
                pltpu.VMEM((3, WINDOW, TILE), BF16),
                pltpu.VMEM((PADDED, LANES), BF16),
                pltpu.VMEM((PADDED, PADDED), BF16),
                pltpu.VMEM((2, PADDED, PADDED), BF16),
                pltpu.VMEM((2, TILE, TILE), BF16),
                pltpu.VMEM((16, PADDED), F32),
                pltpu.VMEM((TILE // LANES, 3, LANES + 2 * RIM, LANES), F32),
                pltpu.VMEM((16, TILE), F32),
                pltpu.VMEM((16, TILE), F32),
                pltpu.VMEM((16, TILE), F32),
            ],
        ),
        out_shape=jax.ShapeDtypeStruct((tiles, 8, TILE), F32),
        name="correlate",
    )(offsets, left, right, right, right, above, below, west, east)


def bin_kernel(
    per_owner, obs_ref, owner_ref, source_ref, line_ref, out_ref, value_ref, spot_ref, hot_ref, part_ref, bins_ref
):
    tiles = obs_ref.shape[0]
    groups = owner_ref.shape[0] // 8
    match_rows = hot_ref.shape[1] // LANES
    bins = bins_ref.shape[1]
    sources = [source_ref[8 * g : 8 * g + 8, :] for g in range(groups)]
    high = [source // LANES for source in sources]
    low = [source % LANES for source in sources]
    fields = [[jnp.zeros((8, LANES), F32)] * groups for _ in range(3)]
    for t in range(tiles):
        for b in range(TILE // LANES):
            here = [h == t * (TILE // LANES) + b for h in high]
            for v in range(3):
                table = jnp.broadcast_to(
                    obs_ref[t, v : v + 1, LANES * b : LANES * (b + 1)], (8, LANES)
                )
                for g in range(groups):
                    taken = jnp.take_along_axis(table, low[g], axis=1, mode="promise_in_bounds")
                    fields[v][g] = jnp.where(here[g], taken, fields[v][g])
    for g in range(groups):
        rows = slice(8 * g, 8 * g + 8)
        line = line_ref[rows, :]
        far = ((line % SAMP).astype(F32) + 0.5) / SAMP
        near = 1.0 - far
        sample = owner_ref[rows, :] * per_owner + line // SAMP
        spot_ref[0, rows, :] = sample // LANES
        spot_ref[1, rows, :] = sample % LANES
        weight = fields[2][g]
        along, across = weight * fields[0][g], weight * fields[1][g]
        values = [
            weight * (near * near),
            weight * (far * far),
            weight * (far * near),
            along * near,
            along * far,
            across * near,
            across * far,
        ]
        for v in range(7):
            upper = values[v].astype(BF16).astype(F32)
            value_ref[v, 0, rows, :] = upper
            value_ref[v, 1, rows, :] = values[v] - upper
    for r in range(match_rows):
        hot = iota((LANES, LANES), 0) == spot_ref[1, r : r + 1, :]
        hot_ref[:, LANES * r : LANES * (r + 1)] = hot.astype(F32).astype(BF16)

    @pl.loop(0, 7)
    def _(v):
        for r in range(match_rows):
            here = iota((bins, LANES), 0) == spot_ref[0, r : r + 1, :]
            for p in range(2):
                part_ref[p, :, LANES * r : LANES * (r + 1)] = jnp.where(
                    here, value_ref[v, p, r : r + 1, :], 0.0
                ).astype(BF16)
        contract = (((1,), (1,)), ((), ()))
        bins_ref[v] = lax.dot_general(
            part_ref[0], hot_ref[...], contract, preferred_element_type=F32
        ) + lax.dot_general(part_ref[1], hot_ref[...], contract, preferred_element_type=F32)

    lane, row = iota((bins, LANES), 1), iota((bins, LANES), 0)
    for v in (1, 4, 6):
        turned = pltpu.roll(bins_ref[v], 1, 1)
        carried = jnp.where(row == 0, 0.0, pltpu.roll(turned, 1, 0))
        bins_ref[v - 1] = bins_ref[v - 1] + jnp.where(lane == 0, carried, turned)
    span = per_owner // LANES
    for d in range(bins // span):
        for i, v in enumerate((0, 2, 3, 5)):
            out_ref[d, span * i : span * (i + 1), :] = bins_ref[v, span * d : span * (d + 1), :]


def bin_matches(observations, owner, source, line, device_count, per_owner):
    count = source.shape[0]
    match_rows = count // LANES
    padded_rows = -(-match_rows // 8) * 8
    spare = padded_rows * LANES - count

    def lay(array, fill):
        return jnp.pad(array, (0, spare), constant_values=fill).reshape(padded_rows, LANES)

    bins = device_count * per_owner // LANES
    block = 4 * per_owner // LANES
    return pl.pallas_call(
        functools.partial(bin_kernel, per_owner),
        out_shape=jax.ShapeDtypeStruct((device_count, block, LANES), F32),
        scratch_shapes=[
            pltpu.VMEM((7, 2, padded_rows, LANES), F32),
            pltpu.VMEM((2, padded_rows, LANES), jnp.int32),
            pltpu.VMEM((LANES, match_rows * LANES), BF16),
            pltpu.VMEM((2, bins, match_rows * LANES), BF16),
            pltpu.VMEM((7, bins, LANES), F32),
        ],
        name="bin_matches",
    )(observations, lay(owner, 0), lay(source, 0), lay(line, 0))


def local(left_image, right_image, peak_offsets, match_owner, match_source, match_line):
    rows_dev = left_image.shape[0]
    seg_count = lax.axis_size("seg")
    col_count = lax.axis_size("col")
    device_count = seg_count * col_count
    samp_own = rows_dev // (SAMP * col_count)

    def forward(value, axis):
        size = lax.axis_size(axis)
        return lax.ppermute(value, axis, [(i, i + 1) for i in range(size - 1)])

    def backward(value, axis):
        size = lax.axis_size(axis)
        return lax.ppermute(value, axis, [(i + 1, i) for i in range(size - 1)])

    above = forward(right_image[rows_dev - RIM :], "seg")
    below = backward(right_image[:RIM], "seg")
    first_edge, last_edge = edges(right_image, above, below)
    west = forward(last_edge, "col")
    east = backward(first_edge, "col")
    observations = correlate(
        peak_offsets[:, :, 0], left_image, right_image, above, below, west, east
    )
    outgoing = bin_matches(
        observations, match_owner[:, 0], match_source, match_line, device_count, samp_own
    )
    received = lax.all_to_all(outgoing, ("seg", "col"), split_axis=0, concat_axis=0, tiled=True)
    by_column = jnp.sum(received.reshape(seg_count, col_count, 4, samp_own), axis=0)
    index_pairs = ((0, 0), (0, 1), (0, 2), (1, 1), (1, 2), (2, 2))
    diagonal, coupling, right_side = [0.0] * 6, [0.0] * 6, [0.0] * 3
    for column in range(col_count):
        spread = 2.0 * (column + 0.5) / col_count - 1.0
        along = (JACOBIAN_A * spread, 1.0, spread)
        across = (1.0, JACOBIAN_B * spread, JACOBIAN_C * spread)
        near, both, resid_row, resid_col = (by_column[column, i] for i in range(4))
        for i, (a, b) in enumerate(index_pairs):
            factor = along[a] * along[b] + across[a] * across[b]
            diagonal[i] = diagonal[i] + factor * near
            coupling[i] = coupling[i] + factor * both
        for a in range(3):
            right_side[a] = right_side[a] + along[a] * resid_row + across[a] * resid_col
    return (jnp.stack(diagonal), jnp.stack(coupling), jnp.stack(right_side))


def solution(mesh):
    return jax.shard_map(
        local,
        mesh=mesh,
        in_specs=(
            P("seg", "col"),
            P("seg", "col"),
            P(None, "seg", "col"),
            P(("seg", "col"), None),
            P(("seg", "col")),
            P(("seg", "col")),
        ),
        out_specs=(P(None, ("seg", "col")), P(None, ("seg", "col")), P(None, ("seg", "col"))),
        check_vma=False,
    )
```
